256 devices in a mesh: pipe: 4 (over z_lo), expert: 64 (over y, z_hi, x, core).
Axes of the slice: x: 4, y: 4, z: 8 (z_hi: 2, z_lo: 4; z = z_hi * 4 + z_lo), core: 2. Of those that a mesh axis runs over, the one named last changes fastest.
Arguments:
- tokens: bfloat16 [32768, 3584], P(('pipe', 'expert')), may hold values from -6 to 6
- out_grad: bfloat16 [32768, 3584], P(('pipe', 'expert')), may hold values from -6 to 6
- probs: bfloat16 [32768, 8], P(('pipe', 'expert')), may hold values from 0.049804688 to 1
- expert_ids: int32 [32768, 8], P(('pipe', 'expert')), may hold values from 0 to 255, as said below
- w_gate: bfloat16 [4, 3584, 16384], P('pipe', None, 'expert'), as said below
- w_up: bfloat16 [4, 3584, 16384], P('pipe', None, 'expert'), as said below
- w_down: bfloat16 [4, 16384, 3584], P('pipe', 'expert'), as said below
Outputs:
- tokens_grad: bfloat16 [32768, 3584], P(('pipe', 'expert'))
- weight_grads: bfloat16 [4, 3, 1792, 16384], P('pipe', None, None, 'expert')
The draws below stay inside these ranges and needn't reach their ends.
Inputs may be any that keep to these rules, and one draw needn't show every extreme that they name: `expert_ids`: each row names 8 different experts. Experts 8 and above lie outside this window. Among the 128 tokens of one device (aligned blocks of rows), each expert below 8 is named by at most 8 tokens, and in every draw one such expert is named by exactly 8 tokens on every device. `w_gate`: entries k and 3 - k along the first dimension are equal. `w_up`: entries k and 3 - k along the first dimension are equal. `w_down`: entries k and 3 - k along the first dimension are equal.
All inputs are finite; a program needn't handle non-finite values.
Results may differ from the reference program's by a relative error of at most 0.0065.
Values may be sent and summed in bfloat16 or wider, within the bound.
No kernel may reach another device: no remote copies, remote signals or barrier semaphores. Data moves between devices by JAX's collectives and lax.ppermute only.
A program may use at most 128 MiB of HBM per device.

```python
import math
import jax
import jax.numpy as jnp
from jax import lax

D = 3584
H = 2048
EXPERTS = 256
TOP = 8
TOK_DEV = 128
CAP = 8
EXP_FLIGHT = 8
TOKENS = 32768
N_PIPE = 4
N_EXPERT = 64


def draw_expert_ids(key, part):
    blocks = TOKENS // TOK_DEV
    key_hot, key_count, key_order, key_offset, key_turn = jax.random.split(key, 5)
    hottest = jax.random.randint(key_hot, (), 0, EXP_FLIGHT)
    counts = jax.random.randint(key_count, (blocks, EXP_FLIGHT), 0, CAP + 1)
    counts = jnp.where(jnp.arange(EXP_FLIGHT)[None, :] == hottest, CAP, counts)
    order_keys = jax.random.split(key_order, blocks * EXP_FLIGHT)
    orders = jax.vmap(lambda single: jax.random.permutation(single, TOK_DEV))(order_keys)
    orders = orders.reshape(blocks, EXP_FLIGHT, TOK_DEV)
    chosen = orders < counts[:, :, None]
    chosen = jnp.transpose(chosen, (0, 2, 1)).reshape(TOKENS, EXP_FLIGHT)
    chosen = jnp.pad(chosen, ((0, 0), (0, TOP - EXP_FLIGHT)))
    outside = EXPERTS - EXP_FLIGHT
    offset = jax.random.randint(key_offset, (TOKENS, 1), 0, outside)
    column = jnp.arange(TOP)[None, :]
    listed = jnp.where(chosen, column, EXP_FLIGHT + (offset + column) % outside)
    turn = jax.random.randint(key_turn, (TOKENS, 1), 0, TOP)
    gather_index = (column - turn) % TOP
    return jnp.take_along_axis(listed, gather_index, axis=1).astype(jnp.int32)


def mirrored_weight(key, rows, columns, fan_in):
    sections = N_PIPE // 2
    base = jax.random.normal(key, (sections, rows, columns), jnp.float32) * float(fan_in) ** (-0.5)
    ranks = jnp.arange(N_PIPE)
    section_of = jnp.minimum(ranks, N_PIPE - 1 - ranks)
    return base[section_of]


def draw_w_gate(key, part):
    return mirrored_weight(jax.random.fold_in(key, 11), D, EXP_FLIGHT * H, D).astype(jnp.bfloat16)


def draw_w_up(key, part):
    return mirrored_weight(jax.random.fold_in(key, 23), D, EXP_FLIGHT * H, D).astype(jnp.bfloat16)


def draw_w_down(key, part):
    return mirrored_weight(jax.random.fold_in(key, 37), EXP_FLIGHT * H, D, H).astype(jnp.bfloat16)


def shard_levels(rng, shape, shards, least, high):
    loudness = 1.0
    for dim, parts in shards:
        heights = jax.random.uniform(jax.random.fold_in(jax.random.fold_in(rng, 6), dim), (parts,), jnp.float32, least / len(shards), high / len(shards))
        loudness = loudness * jnp.repeat(jnp.exp(heights), shape[dim] // parts).reshape((-1,) + (1,) * (len(shape) - 1 - dim))
    return loudness


def centred(rng, shape, deviation, bound, cuts=(), kind=jnp.bfloat16):
    values = deviation * jax.random.normal(rng, shape, jnp.float32)
    if cuts:
        values = values * shard_levels(rng, shape, cuts, -0.22, 0.18)
    return jnp.clip(values, -bound, bound).astype(kind)


def setup_inputs(seed: int = 0) -> dict:
    splits = jax.random.split(jax.random.key(seed), 8)
    tokens = centred(splits[0], (TOKENS, D), 1.0, 6.0, ((0, 256),))
    out_grad = centred(splits[1], (TOKENS, D), 1.0, 6.0, ((0, 256),))
    probs = jnp.clip(jnp.exp(math.log(1.0) - 2.9996462 * jax.random.uniform(splits[2], (TOKENS, TOP), jnp.float32) ** shard_levels(splits[2], (TOKENS, TOP), ((0, 256),), -0.2, 0.2)), 0.049804688, 1.0).astype(jnp.bfloat16)
    expert_ids = draw_expert_ids(jax.random.fold_in(splits[7], 71), 0)
    w_gate = draw_w_gate(jax.random.fold_in(splits[7], 71), 0)
    w_up = draw_w_up(jax.random.fold_in(splits[7], 71), 0)
    w_down = draw_w_down(jax.random.fold_in(splits[7], 71), 0)
    return dict(tokens=tokens, out_grad=out_grad, probs=probs, expert_ids=expert_ids, w_gate=w_gate, w_up=w_up, w_down=w_down)


def route_slots(block_ids, block_probs, in_flight):
    experts = jnp.arange(in_flight, dtype=jnp.int32)
    hits = block_ids[:, :, None] == experts[None, None, :]
    member = jnp.any(hits, axis=1).astype(jnp.int32)
    chosen = jnp.sum(jnp.where(hits, block_probs.astype(jnp.float32)[:, :, None], jnp.float32(0.0)), axis=1)
    position = (jnp.cumsum(member, axis=0) - member).astype(jnp.int32)
    slots = jnp.arange(CAP, dtype=jnp.int32)
    select = (member.T[:, None, :] == 1) & (position.T[:, None, :] == slots[None, :, None])
    select = select.astype(jnp.float32)
    slot_weight = jnp.einsum("ect,te->ec", select, chosen, precision=lax.Precision.HIGHEST)
    return select.reshape(in_flight * CAP, -1), slot_weight.reshape(in_flight * CAP)


def expert_backward(operands):
    x_rows, grad_rows, gate_cols, up_cols, down_rows = operands
    gate = jnp.dot(x_rows, gate_cols, preferred_element_type=jnp.float32)
    up = jnp.dot(x_rows, up_cols, preferred_element_type=jnp.float32)
    sigmoid_gate = jax.nn.sigmoid(gate)
    activated = gate * sigmoid_gate
    hidden = (activated * up).astype(jnp.bfloat16)
    back = jnp.dot(grad_rows, down_rows.T, preferred_element_type=jnp.float32)
    d_gate = (back * up * sigmoid_gate * (1.0 + gate * (1.0 - sigmoid_gate))).astype(jnp.bfloat16)
    d_up = (back * activated).astype(jnp.bfloat16)
    row_grad = jnp.dot(d_gate, gate_cols.T, preferred_element_type=jnp.float32) + jnp.dot(d_up, up_cols.T, preferred_element_type=jnp.float32)
    grads = jnp.stack([
        jnp.dot(x_rows.T, d_gate, preferred_element_type=jnp.float32),
        jnp.dot(x_rows.T, d_up, preferred_element_type=jnp.float32),
        jnp.dot(grad_rows.T, hidden, preferred_element_type=jnp.float32),
    ]).astype(jnp.bfloat16)
    return row_grad, grads


def reference(tokens, out_grad, probs, expert_ids, w_gate, w_up, w_down):
    in_flight = EXP_FLIGHT
    blocks = N_PIPE * N_EXPERT

    def prepare(block_tokens, block_grad, block_probs, block_ids):
        select, slot_weight = route_slots(block_ids, block_probs, in_flight)
        picker = select.astype(jnp.bfloat16)
        x_rows = jnp.dot(picker, block_tokens, preferred_element_type=jnp.float32).astype(jnp.bfloat16)
        grad_rows = (jnp.dot(picker, block_grad, preferred_element_type=jnp.float32) * slot_weight[:, None]).astype(jnp.bfloat16)
        return select, x_rows, grad_rows

    select, x_rows, grad_rows = jax.vmap(prepare)(
        tokens.reshape(blocks, TOK_DEV, D), out_grad.reshape(blocks, TOK_DEV, D),
        probs.reshape(blocks, TOK_DEV, TOP), expert_ids.reshape(blocks, TOK_DEV, TOP))

    def by_expert(rows):
        rows = rows.reshape(N_PIPE, N_EXPERT, in_flight, CAP, D).transpose(0, 2, 1, 3, 4)
        return rows.reshape(N_PIPE * in_flight, N_EXPERT * CAP, D)

    gate_cols = w_gate.reshape(N_PIPE, D, in_flight, H).transpose(0, 2, 1, 3).reshape(N_PIPE * in_flight, D, H)
    up_cols = w_up.reshape(N_PIPE, D, in_flight, H).transpose(0, 2, 1, 3).reshape(N_PIPE * in_flight, D, H)
    down_rows = w_down.reshape(N_PIPE * in_flight, H, D)
    row_grad, grads = lax.map(expert_backward, (by_expert(x_rows), by_expert(grad_rows), gate_cols, up_cols, down_rows))

    row_grad = row_grad.reshape(N_PIPE, in_flight, N_EXPERT, CAP, D).transpose(0, 2, 1, 3, 4).reshape(blocks, in_flight * CAP, D)
    tokens_grad = jnp.einsum("bst,bsd->btd", select, row_grad, precision=lax.Precision.HIGHEST)
    tokens_grad = tokens_grad.astype(jnp.bfloat16).reshape(TOKENS, D)

    grads = grads.reshape(N_PIPE, in_flight, 3, D, H).transpose(0, 2, 3, 1, 4).reshape(N_PIPE, 3, D, in_flight * H)
    mirrored = grads[::-1]
    half_rows = D // 2
    half_pipe = N_PIPE // 2
    lower = (grads[:half_pipe, :, :half_rows].astype(jnp.float32) + mirrored[:half_pipe, :, :half_rows].astype(jnp.float32)).astype(jnp.bfloat16)
    upper = (grads[half_pipe:, :, half_rows:].astype(jnp.float32) + mirrored[half_pipe:, :, half_rows:].astype(jnp.float32)).astype(jnp.bfloat16)
    weight_grads = jnp.concatenate([lower, upper], axis=0)
    return tokens_grad, weight_grads
```

```python
import jax
import jax.numpy as jnp
from jax import lax
from jax.sharding import PartitionSpec as P

GROUP = 8
CAP = 8
CORES = 2
CHIPS = GROUP // CORES


def route_slots(block_ids, block_probs, in_flight):
    experts = jnp.arange(in_flight, dtype=jnp.int32)
    hits = block_ids[:, :, None] == experts[None, None, :]
    member = jnp.any(hits, axis=1).astype(jnp.int32)
    chosen = jnp.sum(
        jnp.where(hits, block_probs.astype(jnp.float32)[:, :, None], jnp.float32(0.0)), axis=1
    )
    position = jnp.cumsum(member, axis=0) - member
    slots = jnp.arange(CAP, dtype=jnp.int32)
    select = (member.T[:, None, :] == 1) & (position.T[:, None, :] == slots[None, :, None])
    select = select.astype(jnp.float32)
    slot_weight = jnp.einsum("ect,te->ec", select, chosen, precision=lax.Precision.HIGHEST)
    return (select.reshape(in_flight * CAP, -1), slot_weight.reshape(in_flight * CAP))


def contract(left, right, left_dim, right_dim):
    return lax.dot_general(
        left, right, (((left_dim,), (right_dim,)), ((), ())), preferred_element_type=jnp.float32
    )


def along_x(value, shift):
    width = lax.axis_size("expert")
    pairs = []
    for source in range(width):
        group, member = divmod(source, GROUP)
        chip, core = divmod(member, CORES)
        pairs.append((source, group * GROUP + (chip + shift) % CHIPS * CORES + core))
    return lax.ppermute(value, "expert", pairs)


def other_core(value):
    width = lax.axis_size("expert")
    return lax.ppermute(value, "expert", [(source, source ^ 1) for source in range(width)])


def mirror(value):
    count = lax.axis_size("pipe")
    return lax.ppermute(value, "pipe", [(k, count - 1 - k) for k in range(count)])


def across_groups(value):
    width = lax.axis_size("expert")
    groups = [[e * GROUP + g for e in range(width // GROUP)] for g in range(GROUP)]
    return lax.all_to_all(
        value, "expert", split_axis=0, concat_axis=0, axis_index_groups=groups, tiled=True
    )


def gather_chips(rows):
    half = rows.shape[0] // 2
    below = along_x(rows, 1)
    above = along_x(rows, -1)
    far_low = along_x(below[:half], 1)
    far_high = along_x(above[half:], -1)
    return jnp.concatenate([rows, below, above, far_low, far_high])


def body(tokens, out_grad, probs, expert_ids, w_gate, w_up, w_down):
    axis_width = lax.axis_size("expert")
    in_flight = axis_width // GROUP
    features = tokens.shape[1]
    half_rows = features // 2
    lower = lax.axis_index("pipe") < lax.axis_size("pipe") // 2
    w_gate, w_up, w_down = w_gate[0], w_up[0], w_down[0]
    bf16 = jnp.bfloat16

    select, slot_weight = route_slots(expert_ids, probs, in_flight)
    picker = select.astype(bf16)
    x_rows = jnp.dot(picker, tokens, preferred_element_type=jnp.float32).astype(bf16)
    grad_rows = (
        jnp.dot(picker, out_grad, preferred_element_type=jnp.float32) * slot_weight[:, None]
    ).astype(bf16)

    x_here = across_groups(x_rows)
    g_here = across_groups(grad_rows)

    def keep(value):
        return jnp.where(lower, value[:, :half_rows], value[:, half_rows:])

    def give(value):
        return jnp.where(lower, value[:, half_rows:], value[:, :half_rows])

    x_mine = gather_chips(x_here)
    x_other = other_core(x_mine)
    g_mine = gather_chips(g_here)
    g_other = other_core(g_mine)
    m_here = mirror(jnp.concatenate([give(x_here), give(g_here)], axis=1))
    m_mine = gather_chips(m_here)
    m_other = other_core(m_mine)

    def hidden_units(x, g):
        gate = jnp.dot(x, w_gate, preferred_element_type=jnp.float32)
        up = jnp.dot(x, w_up, preferred_element_type=jnp.float32)
        back = contract(g, w_down, 1, 1)
        s = jax.nn.sigmoid(gate)
        activated = gate * s
        hidden = (activated * up).astype(bf16)
        d_gate = (back * up * s * (1.0 + gate * (1.0 - s))).astype(bf16)
        d_up = (back * activated).astype(bf16)
        return d_gate, d_up, hidden

    x_all = jnp.concatenate([x_mine, x_other])
    g_all = jnp.concatenate([g_mine, g_other])
    d_gate, d_up, hidden = hidden_units(x_all, g_all)
    acts = jnp.stack([d_gate, d_up, hidden])
    m_acts = mirror(acts)

    row_grad = contract(d_gate, w_gate, 1, 1) + contract(d_up, w_up, 1, 1)
    n_mine = x_mine.shape[0]
    rows_dev = n_mine // CHIPS
    summed = row_grad[:n_mine] + other_core(row_grad[n_mine:].astype(bf16)).astype(jnp.float32)
    to_below = summed[rows_dev : 2 * rows_dev].astype(bf16)
    to_above = summed[2 * rows_dev : 3 * rows_dev].astype(bf16)
    to_far = summed[3 * rows_dev :].astype(bf16)
    total = (
        summed[:rows_dev]
        + along_x(to_below, -1).astype(jnp.float32)
        + along_x(to_above, 1).astype(jnp.float32)
        + along_x(to_far, 2).astype(jnp.float32)
    )
    returned = across_groups(total.astype(bf16))
    tokens_grad = contract(picker, returned, 0, 0).astype(bf16)

    x_keep = jnp.concatenate([keep(x_all), m_mine[:, :half_rows], m_other[:, :half_rows]])
    g_keep = jnp.concatenate([keep(g_all), m_mine[:, half_rows:], m_other[:, half_rows:]])
    both = jnp.concatenate([acts, m_acts], axis=1)
    weight_grads = jnp.stack(
        [
            contract(x_keep, both[0], 0, 0).astype(bf16),
            contract(x_keep, both[1], 0, 0).astype(bf16),
            contract(g_keep, both[2], 0, 0).astype(bf16),
        ]
    )
    return (tokens_grad, weight_grads[None])


def solution(mesh):
    return jax.shard_map(
        body,
        mesh=mesh,
        in_specs=(
            P(("pipe", "expert"), None),
            P(("pipe", "expert"), None),
            P(("pipe", "expert"), None),
            P(("pipe", "expert"), None),
            P("pipe", None, "expert"),
            P("pipe", None, "expert"),
            P("pipe", "expert", None),
        ),
        out_specs=(P(("pipe", "expert"), None), P("pipe", None, None, "expert")),
        check_vma=False,
    )
```

```python
import jax
import jax.numpy as jnp
from jax import lax
from jax.experimental import pallas as pl
from jax.experimental.pallas import tpu as pltpu
from jax.sharding import PartitionSpec as P

GROUP = 8
CAP = 8
CORES = 2
CHIPS = GROUP // CORES
BF16 = jnp.bfloat16
F32 = jnp.float32


def dot(left, right, left_dim, right_dim):
    return lax.dot_general(
        left, right, (((left_dim,), (right_dim,)), ((), ())), preferred_element_type=F32
    )


def cost(microseconds):
    return pl.CostEstimate(
        flops=int(microseconds * 1.0e9), transcendentals=0, bytes_accessed=int(microseconds * 1.0e6)
    )


def run(kernel, outs, *operands, scalars=0, limit=8, us=1.0):
    vmem = pl.BlockSpec(memory_space=pltpu.VMEM)
    smem = pl.BlockSpec(memory_space=pltpu.SMEM)
    return pl.pallas_call(
        kernel,
        out_shape=[jax.ShapeDtypeStruct(shape, dtype) for shape, dtype in outs],
        in_specs=[smem] * scalars + [vmem] * (len(operands) - scalars),
        out_specs=[vmem] * len(outs),
        compiler_params=pltpu.CompilerParams(vmem_limit_bytes=limit << 20),
        cost_estimate=cost(us),
    )(*operands)


def route_kernel(upper, tokens, out_grad, probs, ids, x_rows, sent, select):
    count, top = ids.shape
    experts = x_rows.shape[0] // CAP
    ids = ids[...]
    probs = probs[...].astype(F32)
    lane = lax.broadcasted_iota(jnp.int32, (count, experts), 1)
    member = jnp.zeros((count, experts), F32)
    chosen = jnp.zeros((count, experts), F32)
    for k in range(top):
        hit = ids[:, k : k + 1] == lane
        member = jnp.where(hit, 1.0, member)
        chosen = chosen + jnp.where(hit, probs[:, k : k + 1], 0.0)
    row = lax.broadcasted_iota(jnp.int32, (count, count), 0)
    col = lax.broadcasted_iota(jnp.int32, (count, count), 1)
    earlier = jnp.where(col < row, 1.0, 0.0).astype(BF16)
    position = dot(earlier, member.astype(BF16), 1, 0)
    slots = experts * CAP
    expert_of = lax.broadcasted_iota(jnp.int32, (experts, slots), 1) // CAP
    spread = jnp.where(
        expert_of == lax.broadcasted_iota(jnp.int32, (experts, slots), 0), 1.0, 0.0
    ).astype(BF16)
    member = dot(member.astype(BF16), spread, 1, 0)
    position = dot(position.astype(BF16), spread, 1, 0)
    chosen = dot(chosen.astype(BF16), spread, 1, 0)
    slot = (lax.broadcasted_iota(jnp.int32, (count, slots), 1) % CAP).astype(F32)
    picked = (member == 1.0) & (position == slot)
    sel = jnp.where(picked, 1.0, 0.0).astype(BF16)
    weights = jnp.where(picked, chosen, 0.0).astype(BF16)
    weight = dot(weights, jnp.ones((count, 128), BF16), 0, 0)[:, :1]
    select[...] = sel
    x = dot(sel, tokens[...], 0, 0).astype(BF16)
    g = (dot(sel, out_grad[...], 0, 0) * weight).astype(BF16)
    x_rows[...] = x
    half = x.shape[1] // 2
    high = upper[0] == 1
    own_at = pl.ds(pl.multiple_of(upper[0] * slots, slots), slots)
    mirror_at = pl.ds(pl.multiple_of((1 - upper[0]) * slots, slots), slots)
    sent[own_at, :] = g
    sent[mirror_at, :half] = jnp.where(high, x[:, :half], x[:, half:])
    sent[mirror_at, half:] = jnp.where(high, g[:, :half], g[:, half:])


def split_kernel(upper, arrived, g_here, m_here):
    n = g_here.shape[0]
    g_here[...] = arrived[pl.ds(pl.multiple_of(upper[0] * n, n), n), :]
    m_here[...] = arrived[pl.ds(pl.multiple_of((1 - upper[0]) * n, n), n), :]


def pack_kernel(a, b, c, d, out):
    n = a.shape[0]
    for i, piece in enumerate((a, b, c, d)):
        out[i * n : (i + 1) * n, :] = piece[...]


def up_kernel(x_mine, x_other, w_gate, w_up, gate, up):
    n = x_mine.shape[0]
    for i, x in enumerate((x_mine, x_other)):
        at = slice(i * n, (i + 1) * n)
        gate[at, :] = dot(x[...], w_gate[0], 1, 0)
        up[at, :] = dot(x[...], w_up[0], 1, 0)


def back_kernel(g_mine, g_other, w_down, gate, up, acts):
    n = g_mine.shape[0]
    for i, g in enumerate((g_mine, g_other)):
        at = slice(i * n, (i + 1) * n)
        back = dot(g[...], w_down[0], 1, 1)
        v, u = gate[at, :], up[at, :]
        s = jax.nn.sigmoid(v)
        activated = v * s
        acts[0, at, :] = (back * u * s * (1.0 + v * (1.0 - s))).astype(BF16)
        acts[1, at, :] = (back * activated).astype(BF16)
        acts[2, at, :] = (activated * u).astype(BF16)


def row_other_kernel(acts, w_gate, w_up, out):
    n = out.shape[0]
    out[...] = (
        dot(acts[0, n:, :], w_gate[0], 1, 1) + dot(acts[1, n:, :], w_up[0], 1, 1)
    ).astype(BF16)


def row_mine_kernel(acts, w_gate, w_up, arrived, own, near, next_, far):
    n, rows = own.shape[0], arrived.shape[0]
    total = dot(acts[0, :rows, :], w_gate[0], 1, 1) + dot(acts[1, :rows, :], w_up[0], 1, 1)
    total = total + arrived[...].astype(F32)
    for i, out in enumerate((own, near, next_, far)):
        out[...] = total[i * n : (i + 1) * n].astype(out.dtype)


def total_kernel(own, near, next_, far, out):
    out[...] = (
        own[...] + near[...].astype(F32) + next_[...].astype(F32) + far[...].astype(F32)
    ).astype(BF16)


def tokens_kernel(select, rows, out):
    out[...] = dot(select[...], rows[...], 1, 0).astype(BF16)


def weights_kernel(upper, xm, xo, gm, go, mxm, mxo, mgm, mgo, acts, m_acts, out):
    x = jnp.concatenate([xm[...], xo[...], mxm[...], mxo[...]])
    g = jnp.concatenate([gm[...], go[...], mgm[...], mgo[...]])
    for i, rows in enumerate((x, x, g)):
        d = jnp.concatenate([acts[i], m_acts[i]])
        out[0, i] = dot(rows, d, 0, 0).astype(BF16)


def weight_grads_of(upper, x_mine, x_other, g_mine, g_other, m_mine, m_other, *acts):
    rows, features = x_mine.shape
    units = acts[0].shape[2]
    tile = 256
    steps = features // 2 // tile
    kept = pl.BlockSpec((rows, tile), lambda i, s: (0, s[0] * steps + i))
    first = pl.BlockSpec((rows, tile), lambda i, s: (0, i))
    second = pl.BlockSpec((rows, tile), lambda i, s: (0, steps + i))
    whole = pl.BlockSpec(acts[0].shape, lambda i, s: (0, 0, 0))
    return pl.pallas_call(
        weights_kernel,
        out_shape=jax.ShapeDtypeStruct((1, 3, features // 2, units), BF16),
        grid_spec=pltpu.PrefetchScalarGridSpec(
            num_scalar_prefetch=1,
            grid=(steps,),
            in_specs=[kept] * 4 + [first] * 2 + [second] * 2 + [whole] * 2,
            out_specs=pl.BlockSpec((1, 3, tile, units), lambda i, s: (0, 0, i, 0)),
        ),
        compiler_params=pltpu.CompilerParams(vmem_limit_bytes=16 << 20),
        cost_estimate=cost(0.1),
    )(upper, x_mine, x_other, g_mine, g_other, m_mine, m_other, m_mine, m_other, *acts)


def permute_members(value, move):
    width = lax.axis_size("expert")
    pairs = []
    for source in range(width):
        group, member = divmod(source, GROUP)
        chip, core = divmod(member, CORES)
        chip, core = move(chip, core)
        pairs.append((source, group * GROUP + chip % CHIPS * CORES + core))
    return lax.ppermute(value, "expert", pairs)


def outward(value):
    return permute_members(value, lambda chip, core: (chip + 1 - 2 * core, core))


def inward(value):
    return permute_members(value, lambda chip, core: (chip - 1 + 2 * core, core))


def across(value):
    return permute_members(value, lambda chip, core: (chip + 2, core))


def other_core(value):
    return permute_members(value, lambda chip, core: (chip, 1 - core))


def mirror(value):
    count = lax.axis_size("pipe")
    return lax.ppermute(value, "pipe", [(k, count - 1 - k) for k in range(count)])


def across_groups(value):
    width = lax.axis_size("expert")
    groups = [[e * GROUP + g for e in range(width // GROUP)] for g in range(GROUP)]
    return lax.all_to_all(
        value, "expert", split_axis=0, concat_axis=0, axis_index_groups=groups, tiled=True
    )


def after(value, *others):
    return lax.optimization_barrier((value, *others))[0]


def across_sections(value):
    width, count = lax.axis_size("expert"), lax.axis_size("pipe")
    groups = [
        [section * width + e * GROUP + g for section in (k, count - 1 - k) for e in range(width // GROUP)]
        for k in range(count // 2)
        for g in range(GROUP)
    ]
    return lax.all_to_all(
        value, ("pipe", "expert"), split_axis=0, concat_axis=0, axis_index_groups=groups, tiled=True
    )


def pack(*pieces, us=1.0):
    rows, features = pieces[0].shape
    return run(pack_kernel, [((len(pieces) * rows, features), BF16)], *pieces, limit=2, us=us)[0]


def together(*values):
    return lax.optimization_barrier(values)


def body(tokens, out_grad, probs, expert_ids, w_gate, w_up, w_down):
    in_flight = lax.axis_size("expert") // GROUP
    features = tokens.shape[1]
    units = w_gate.shape[2]
    slots = in_flight * CAP
    upper = (lax.axis_index("pipe") >= lax.axis_size("pipe") // 2).astype(jnp.int32)
    upper = upper.reshape(1)
    rows = ((slots, features), BF16)
    x_rows, sent, select = run(
        route_kernel,
        [rows, ((2 * slots, features), BF16), ((tokens.shape[0], slots), BF16)],
        upper,
        tokens,
        out_grad,
        probs,
        expert_ids,
        scalars=1,
    )
    x_here = across_groups(x_rows)
    arrived = across_sections(after(sent, x_here))
    x_near, x_next = together(outward(x_here), inward(x_here))
    x_far = outward(x_near)
    arrived = after(arrived, x_near, x_next, x_far)
    g_here, m_here = run(split_kernel, [rows] * 2, upper, arrived, scalars=1, limit=2)
    x_mine = pack(x_here, x_near, x_next, x_far)
    x_other = other_core(x_mine)
    g_near, g_next, _ = together(outward(g_here), inward(g_here), x_mine)
    g_far = outward(g_near)
    gate_shape = ((2 * x_mine.shape[0], units), F32)
    gate, up = run(up_kernel, [gate_shape] * 2, x_mine, x_other, w_gate, w_up, us=3.0)
    g_far = after(g_far, gate)
    g_mine = pack(g_here, g_near, g_next, g_far)
    g_other = other_core(g_mine)

    m_here = after(m_here, g_far)
    m_near, m_next = outward(m_here), inward(m_here)
    acts_shape = ((3, gate.shape[0], units), BF16)
    acts = run(back_kernel, [acts_shape], g_mine, g_other, w_down, gate, up, us=3.0)[0]
    m_acts = mirror(acts)
    ready, m_near, m_next = together(acts, m_near, m_next)
    part = run(row_other_kernel, [(x_other.shape, BF16)], ready, w_gate, w_up, limit=14)[0]
    part = other_core(part)
    own, near, next_, far = run(
        row_mine_kernel, [(rows[0], F32), rows, rows, rows], ready, w_gate, w_up, part, limit=14
    )
    near, next_, far, m_far = together(
        inward(near), outward(next_), across(far), outward(m_near)
    )
    total = run(total_kernel, [rows], own, near, next_, far)[0]
    m_far, m_acts, _ = together(m_far, m_acts, total)
    m_mine = pack(m_here, m_near, m_next, m_far, us=10.0)
    m_other = other_core(m_mine)
    returned = across_groups(total)
    weight_grads = weight_grads_of(
        upper, x_mine, x_other, g_mine, g_other, m_mine, m_other, acts, m_acts
    )
    returned, weight_grads = together(returned, weight_grads)
    tokens_grad = run(tokens_kernel, [(tokens.shape, BF16)], select, returned)[0]
    return (tokens_grad, weight_grads)


def solution(mesh):
    return jax.shard_map(
        body,
        mesh=mesh,
        in_specs=(
            P(("pipe", "expert"), None),
            P(("pipe", "expert"), None),
            P(("pipe", "expert"), None),
            P(("pipe", "expert"), None),
            P("pipe", None, "expert"),
            P("pipe", None, "expert"),
            P("pipe", "expert", None),
        ),
        out_specs=(P(("pipe", "expert"), None), P("pipe", None, None, "expert")),
        check_vma=False,
    )
```

```python
import jax
import jax.numpy as jnp
from jax import lax
from jax.experimental import pallas as pl
from jax.experimental.pallas import tpu as pltpu
from jax.sharding import PartitionSpec as P

GROUP = 8
CAP = 8
CORES = 2
CHIPS = GROUP // CORES
BF16 = jnp.bfloat16
F32 = jnp.float32


def dot(left, right, left_dim, right_dim):
    return lax.dot_general(
        left, right, (((left_dim,), (right_dim,)), ((), ())), preferred_element_type=F32
    )


def cost(microseconds):
    return pl.CostEstimate(
        flops=int(microseconds * 1.0e9), transcendentals=0, bytes_accessed=int(microseconds * 1.0e6)
    )


def run(kernel, outs, *operands, scalars=0, limit=8, us=1.0):
    vmem = pl.BlockSpec(memory_space=pltpu.VMEM)
    smem = pl.BlockSpec(memory_space=pltpu.SMEM)
    return pl.pallas_call(
        kernel,
        out_shape=[jax.ShapeDtypeStruct(shape, dtype) for shape, dtype in outs],
        in_specs=[smem] * scalars + [vmem] * (len(operands) - scalars),
        out_specs=[vmem] * len(outs),
        compiler_params=pltpu.CompilerParams(vmem_limit_bytes=limit << 20),
        cost_estimate=cost(us),
    )(*operands)


def route_kernel(upper, tokens, out_grad, probs, ids, x_rows, sent, select):
    count, top = ids.shape
    experts = x_rows.shape[0] // CAP
    ids = ids[...]
    probs = probs[...].astype(F32)
    lane = lax.broadcasted_iota(jnp.int32, (count, experts), 1)
    member = jnp.zeros((count, experts), F32)
    chosen = jnp.zeros((count, experts), F32)
    for k in range(top):
        hit = ids[:, k : k + 1] == lane
        member = jnp.where(hit, 1.0, member)
        chosen = chosen + jnp.where(hit, probs[:, k : k + 1], 0.0)
    row = lax.broadcasted_iota(jnp.int32, (count, count), 0)
    col = lax.broadcasted_iota(jnp.int32, (count, count), 1)
    earlier = jnp.where(col < row, 1.0, 0.0).astype(BF16)
    position = dot(earlier, member.astype(BF16), 1, 0)
    slots = experts * CAP
    expert_of = lax.broadcasted_iota(jnp.int32, (experts, slots), 1) // CAP
    spread = jnp.where(
        expert_of == lax.broadcasted_iota(jnp.int32, (experts, slots), 0), 1.0, 0.0
    ).astype(BF16)
    member = dot(member.astype(BF16), spread, 1, 0)
    position = dot(position.astype(BF16), spread, 1, 0)
    chosen = dot(chosen.astype(BF16), spread, 1, 0)
    slot = (lax.broadcasted_iota(jnp.int32, (count, slots), 1) % CAP).astype(F32)
    picked = (member == 1.0) & (position == slot)
    sel = jnp.where(picked, 1.0, 0.0).astype(BF16)
    weights = jnp.where(picked, chosen, 0.0).astype(BF16)
    weight = dot(weights, jnp.ones((count, 128), BF16), 0, 0)[:, :1]
    select[...] = sel
    x = dot(sel, tokens[...], 0, 0).astype(BF16)
    g = (dot(sel, out_grad[...], 0, 0) * weight).astype(BF16)
    x_rows[...] = x
    half = x.shape[1] // 2
    high = upper[0] == 1
    own_at = pl.ds(pl.multiple_of(upper[0] * slots, slots), slots)
    mirror_at = pl.ds(pl.multiple_of((1 - upper[0]) * slots, slots), slots)
    sent[own_at, :] = g
    sent[mirror_at, :half] = jnp.where(high, x[:, :half], x[:, half:])
    sent[mirror_at, half:] = jnp.where(high, g[:, :half], g[:, half:])


def split_kernel(upper, arrived, g_here, m_here):
    n = g_here.shape[0]
    g_here[...] = arrived[pl.ds(pl.multiple_of(upper[0] * n, n), n), :]
    m_here[...] = arrived[pl.ds(pl.multiple_of((1 - upper[0]) * n, n), n), :]


def pack_kernel(a, b, c, d, out):
    n = a.shape[0]
    for i, piece in enumerate((a, b, c, d)):
        out[i * n : (i + 1) * n, :] = piece[...]


def up_kernel(x_mine, x_other, w_gate, w_up, gate, up):
    n = x_mine.shape[0]
    for i, x in enumerate((x_mine, x_other)):
        at = slice(i * n, (i + 1) * n)
        gate[at, :] = dot(x[...], w_gate[0], 1, 0)
        up[at, :] = dot(x[...], w_up[0], 1, 0)


def back_kernel(g_mine, g_other, w_down, gate, up, acts):
    n = g_mine.shape[0]
    for i, g in enumerate((g_mine, g_other)):
        at = slice(i * n, (i + 1) * n)
        back = dot(g[...], w_down[0], 1, 1)
        v, u = gate[at, :], up[at, :]
        s = jax.nn.sigmoid(v)
        activated = v * s
        acts[0, at, :] = (back * u * s * (1.0 + v * (1.0 - s))).astype(BF16)
        acts[1, at, :] = (back * activated).astype(BF16)
        acts[2, at, :] = (activated * u).astype(BF16)


def row_other_kernel(acts, w_gate, w_up, out):
    n = out.shape[0]
    out[...] = (
        dot(acts[0, n:, :], w_gate[0], 1, 1) + dot(acts[1, n:, :], w_up[0], 1, 1)
    ).astype(BF16)


def row_mine_kernel(acts, w_gate, w_up, arrived, own, near, next_, far):
    n, rows = own.shape[0], arrived.shape[0]
    total = dot(acts[0, :rows, :], w_gate[0], 1, 1) + dot(acts[1, :rows, :], w_up[0], 1, 1)
    total = total + arrived[...].astype(F32)
    for i, out in enumerate((own, near, next_, far)):
        out[...] = total[i * n : (i + 1) * n].astype(out.dtype)


def total_kernel(own, near, next_, far, out):
    out[...] = (
        own[...] + near[...].astype(F32) + next_[...].astype(F32) + far[...].astype(F32)
    ).astype(BF16)


def tokens_kernel(select, rows, out):
    out[...] = dot(select[...], rows[...], 1, 0).astype(BF16)


def weights_kernel(upper, xm, xo, gm, go, mxm, mxo, mgm, mgo, acts, m_acts, out):
    x = jnp.concatenate([xm[...], xo[...], mxm[...], mxo[...]])
    g = jnp.concatenate([gm[...], go[...], mgm[...], mgo[...]])
    for i, rows in enumerate((x, x, g)):
        d = jnp.concatenate([acts[i], m_acts[i]])
        out[0, i] = dot(rows, d, 0, 0).astype(BF16)


def weight_grads_of(upper, x_mine, x_other, g_mine, g_other, m_mine, m_other, *acts):
    rows, features = x_mine.shape
    units = acts[0].shape[2]
    tile = 256
    steps = features // 2 // tile
    kept = pl.BlockSpec((rows, tile), lambda i, s: (0, s[0] * steps + i))
    first = pl.BlockSpec((rows, tile), lambda i, s: (0, i))
    second = pl.BlockSpec((rows, tile), lambda i, s: (0, steps + i))
    whole = pl.BlockSpec(acts[0].shape, lambda i, s: (0, 0, 0))
    return pl.pallas_call(
        weights_kernel,
        out_shape=jax.ShapeDtypeStruct((1, 3, features // 2, units), BF16),
        grid_spec=pltpu.PrefetchScalarGridSpec(
            num_scalar_prefetch=1,
            grid=(steps,),
            in_specs=[kept] * 4 + [first] * 2 + [second] * 2 + [whole] * 2,
            out_specs=pl.BlockSpec((1, 3, tile, units), lambda i, s: (0, 0, i, 0)),
        ),
        compiler_params=pltpu.CompilerParams(vmem_limit_bytes=16 << 20),
        cost_estimate=cost(0.1),
    )(upper, x_mine, x_other, g_mine, g_other, m_mine, m_other, m_mine, m_other, *acts)


def permute_members(value, move):
    width = lax.axis_size("expert")
    pairs = []
    for source in range(width):
        group, member = divmod(source, GROUP)
        chip, core = divmod(member, CORES)
        chip, core = move(chip, core)
        pairs.append((source, group * GROUP + chip % CHIPS * CORES + core))
    return lax.ppermute(value, "expert", pairs)


def outward(value):
    return permute_members(value, lambda chip, core: (chip + 1 - 2 * core, core))


def inward(value):
    return permute_members(value, lambda chip, core: (chip - 1 + 2 * core, core))


def across(value):
    return permute_members(value, lambda chip, core: (chip + 2, core))


def other_core(value):
    return permute_members(value, lambda chip, core: (chip, 1 - core))


def mirror(value):
    count = lax.axis_size("pipe")
    return lax.ppermute(value, "pipe", [(k, count - 1 - k) for k in range(count)])


def across_groups(value):
    width = lax.axis_size("expert")
    groups = [[e * GROUP + g for e in range(width // GROUP)] for g in range(GROUP)]
    return lax.all_to_all(
        value, "expert", split_axis=0, concat_axis=0, axis_index_groups=groups, tiled=True
    )


def after(value, *others):
    return lax.optimization_barrier((value, *others))[0]


def across_sections(value):
    width, count = lax.axis_size("expert"), lax.axis_size("pipe")
    groups = [
        [section * width + e * GROUP + g for section in (k, count - 1 - k) for e in range(width // GROUP)]
        for k in range(count // 2)
        for g in range(GROUP)
    ]
    return lax.all_to_all(
        value, ("pipe", "expert"), split_axis=0, concat_axis=0, axis_index_groups=groups, tiled=True
    )


def pack(*pieces, us=1.0):
    rows, features = pieces[0].shape
    return run(pack_kernel, [((len(pieces) * rows, features), BF16)], *pieces, limit=2, us=us)[0]


def together(*values):
    return lax.optimization_barrier(values)


def body(tokens, out_grad, probs, expert_ids, w_gate, w_up, w_down):
    in_flight = lax.axis_size("expert") // GROUP
    features = tokens.shape[1]
    units = w_gate.shape[2]
    slots = in_flight * CAP
    upper = (lax.axis_index("pipe") >= lax.axis_size("pipe") // 2).astype(jnp.int32)
    upper = upper.reshape(1)
    rows = ((slots, features), BF16)
    x_rows, sent, select = run(
        route_kernel,
        [rows, ((2 * slots, features), BF16), ((tokens.shape[0], slots), BF16)],
        upper,
        tokens,
        out_grad,
        probs,
        expert_ids,
        scalars=1,
    )
    x_here = across_groups(x_rows)
    arrived = across_sections(after(sent, x_here))
    x_near, x_next = together(outward(x_here), inward(x_here))
    x_far = outward(x_near)
    arrived = after(arrived, x_near, x_next, x_far)
    g_here, m_here = run(split_kernel, [rows] * 2, upper, arrived, scalars=1, limit=2)
    x_mine = pack(x_here, x_near, x_next, x_far)
    x_other = other_core(x_mine)
    g_near, g_next, _ = together(outward(g_here), inward(g_here), x_mine)
    g_far = outward(g_near)
    gate_shape = ((2 * x_mine.shape[0], units), F32)
    gate, up = run(up_kernel, [gate_shape] * 2, x_mine, x_other, w_gate, w_up, us=3.0)
    g_far = after(g_far, gate)
    g_mine = pack(g_here, g_near, g_next, g_far)
    g_other = other_core(g_mine)

    m_here = after(m_here, g_far)
    m_near, m_next = outward(m_here), inward(m_here)
    acts_shape = ((3, gate.shape[0], units), BF16)
    acts = run(back_kernel, [acts_shape], g_mine, g_other, w_down, gate, up, us=3.0)[0]
    m_acts = mirror(acts)
    ready, m_near = together(acts, m_near)
    part = run(row_other_kernel, [(x_other.shape, BF16)], ready, w_gate, w_up, limit=14)[0]
    part = other_core(part)
    own, near, next_, far = run(
        row_mine_kernel, [(rows[0], F32), rows, rows, rows], ready, w_gate, w_up, part, limit=14
    )
    near, next_, far, m_far = together(
        inward(near), outward(next_), across(far), outward(m_near)
    )
    total = run(total_kernel, [rows], own, near, next_, far)[0]
    m_far, m_next, m_acts, _ = together(m_far, m_next, m_acts, total)
    m_mine = pack(m_here, m_near, m_next, m_far, us=10.0)
    m_other = other_core(m_mine)
    returned = across_groups(total)
    weight_grads = weight_grads_of(
        upper, x_mine, x_other, g_mine, g_other, m_mine, m_other, acts, m_acts
    )
    returned, weight_grads = together(returned, weight_grads)
    tokens_grad = run(tokens_kernel, [(tokens.shape, BF16)], select, returned)[0]
    return (tokens_grad, weight_grads)


def solution(mesh):
    return jax.shard_map(
        body,
        mesh=mesh,
        in_specs=(
            P(("pipe", "expert"), None),
            P(("pipe", "expert"), None),
            P(("pipe", "expert"), None),
            P(("pipe", "expert"), None),
            P("pipe", None, "expert"),
            P("pipe", None, "expert"),
            P("pipe", "expert", None),
        ),
        out_specs=(P(("pipe", "expert"), None), P("pipe", None, None, "expert")),
        check_vma=False,
    )
```

```python
import jax
import jax.numpy as jnp
from jax import lax
from jax.experimental import pallas as pl
from jax.experimental.pallas import tpu as pltpu
from jax.sharding import PartitionSpec as P

GROUP = 8
CAP = 8
CORES = 2
CHIPS = GROUP // CORES
BF16 = jnp.bfloat16
F32 = jnp.float32


def dot(left, right, left_dim, right_dim):
    return lax.dot_general(
        left, right, (((left_dim,), (right_dim,)), ((), ())), preferred_element_type=F32
    )


def cost(microseconds):
    return pl.CostEstimate(
        flops=int(microseconds * 1.0e9), transcendentals=0, bytes_accessed=int(microseconds * 1.0e6)
    )


def run(kernel, outs, *operands, scalars=0, limit=8, us=1.0):
    vmem = pl.BlockSpec(memory_space=pltpu.VMEM)
    smem = pl.BlockSpec(memory_space=pltpu.SMEM)
    return pl.pallas_call(
        kernel,
        out_shape=[jax.ShapeDtypeStruct(shape, dtype) for shape, dtype in outs],
        in_specs=[smem] * scalars + [vmem] * (len(operands) - scalars),
        out_specs=[vmem] * len(outs),
        compiler_params=pltpu.CompilerParams(vmem_limit_bytes=limit << 20),
        cost_estimate=cost(us),
    )(*operands)


def route_kernel(upper, tokens, out_grad, probs, ids, x_rows, sent, select):
    count, top = ids.shape
    experts = x_rows.shape[0] // CAP
    ids = ids[...]
    probs = probs[...].astype(F32)
    lane = lax.broadcasted_iota(jnp.int32, (count, experts), 1)
    member = jnp.zeros((count, experts), F32)
    chosen = jnp.zeros((count, experts), F32)
    for k in range(top):
        hit = ids[:, k : k + 1] == lane
        member = jnp.where(hit, 1.0, member)
        chosen = chosen + jnp.where(hit, probs[:, k : k + 1], 0.0)
    row = lax.broadcasted_iota(jnp.int32, (count, count), 0)
    col = lax.broadcasted_iota(jnp.int32, (count, count), 1)
    earlier = jnp.where(col < row, 1.0, 0.0).astype(BF16)
    position = dot(earlier, member.astype(BF16), 1, 0)
    slots = experts * CAP
    expert_of = lax.broadcasted_iota(jnp.int32, (experts, slots), 1) // CAP
    spread = jnp.where(
        expert_of == lax.broadcasted_iota(jnp.int32, (experts, slots), 0), 1.0, 0.0
    ).astype(BF16)
    member = dot(member.astype(BF16), spread, 1, 0)
    position = dot(position.astype(BF16), spread, 1, 0)
    chosen = dot(chosen.astype(BF16), spread, 1, 0)
    slot = (lax.broadcasted_iota(jnp.int32, (count, slots), 1) % CAP).astype(F32)
    picked = (member == 1.0) & (position == slot)
    sel = jnp.where(picked, 1.0, 0.0).astype(BF16)
    weights = jnp.where(picked, chosen, 0.0).astype(BF16)
    weight = dot(weights, jnp.ones((count, 128), BF16), 0, 0)[:, :1]
    select[...] = sel
    x = dot(sel, tokens[...], 0, 0).astype(BF16)
    g = (dot(sel, out_grad[...], 0, 0) * weight).astype(BF16)
    x_rows[...] = x
    half = x.shape[1] // 2
    high = upper[0] == 1
    own_at = pl.ds(pl.multiple_of(upper[0] * slots, slots), slots)
    mirror_at = pl.ds(pl.multiple_of((1 - upper[0]) * slots, slots), slots)
    sent[own_at, :] = g
    sent[mirror_at, :half] = jnp.where(high, x[:, :half], x[:, half:])
    sent[mirror_at, half:] = jnp.where(high, g[:, :half], g[:, half:])


def split_kernel(upper, arrived, g_here, m_here):
    n = g_here.shape[0]
    g_here[...] = arrived[pl.ds(pl.multiple_of(upper[0] * n, n), n), :]
    m_here[...] = arrived[pl.ds(pl.multiple_of((1 - upper[0]) * n, n), n), :]


def pack_kernel(a, b, c, d, out):
    n = a.shape[0]
    for i, piece in enumerate((a, b, c, d)):
        out[i * n : (i + 1) * n, :] = piece[...]


def up_kernel(x_mine, x_other, w_gate, w_up, gate, up):
    n = x_mine.shape[0]
    for i, x in enumerate((x_mine, x_other)):
        at = slice(i * n, (i + 1) * n)
        gate[at, :] = dot(x[...], w_gate[0], 1, 0)
        up[at, :] = dot(x[...], w_up[0], 1, 0)


def back_kernel(g_mine, g_other, w_down, gate, up, acts):
    n = g_mine.shape[0]
    for i, g in enumerate((g_mine, g_other)):
        at = slice(i * n, (i + 1) * n)
        back = dot(g[...], w_down[0], 1, 1)
        v, u = gate[at, :], up[at, :]
        s = jax.nn.sigmoid(v)
        activated = v * s
        acts[0, at, :] = (back * u * s * (1.0 + v * (1.0 - s))).astype(BF16)
        acts[1, at, :] = (back * activated).astype(BF16)
        acts[2, at, :] = (activated * u).astype(BF16)


def row_other_kernel(acts, w_gate, w_up, out):
    n = out.shape[0]
    out[...] = (
        dot(acts[0, n:, :], w_gate[0], 1, 1) + dot(acts[1, n:, :], w_up[0], 1, 1)
    ).astype(BF16)


def row_mine_kernel(acts, w_gate, w_up, arrived, own, near, next_, far):
    n, rows = own.shape[0], arrived.shape[0]
    total = dot(acts[0, :rows, :], w_gate[0], 1, 1) + dot(acts[1, :rows, :], w_up[0], 1, 1)
    total = total + arrived[...].astype(F32)
    for i, out in enumerate((own, near, next_, far)):
        out[...] = total[i * n : (i + 1) * n].astype(out.dtype)


def total_kernel(own, near, next_, far, out):
    out[...] = (
        own[...] + near[...].astype(F32) + next_[...].astype(F32) + far[...].astype(F32)
    ).astype(BF16)


def tokens_kernel(select, rows, out):
    out[...] = dot(select[...], rows[...], 1, 0).astype(BF16)


def weights_kernel(upper, xm, xo, gm, go, mxm, mxo, mgm, mgo, acts, m_acts, out):
    x = jnp.concatenate([xm[...], xo[...], mxm[...], mxo[...]])
    g = jnp.concatenate([gm[...], go[...], mgm[...], mgo[...]])
    for i, rows in enumerate((x, x, g)):
        d = jnp.concatenate([acts[i], m_acts[i]])
        out[0, i] = dot(rows, d, 0, 0).astype(BF16)


def weight_grads_of(upper, x_mine, x_other, g_mine, g_other, m_mine, m_other, *acts):
    rows, features = x_mine.shape
    units = acts[0].shape[2]
    tile = 256
    steps = features // 2 // tile
    kept = pl.BlockSpec((rows, tile), lambda i, s: (0, s[0] * steps + i))
    first = pl.BlockSpec((rows, tile), lambda i, s: (0, i))
    second = pl.BlockSpec((rows, tile), lambda i, s: (0, steps + i))
    whole = pl.BlockSpec(acts[0].shape, lambda i, s: (0, 0, 0))
    return pl.pallas_call(
        weights_kernel,
        out_shape=jax.ShapeDtypeStruct((1, 3, features // 2, units), BF16),
        grid_spec=pltpu.PrefetchScalarGridSpec(
            num_scalar_prefetch=1,
            grid=(steps,),
            in_specs=[kept] * 4 + [first] * 2 + [second] * 2 + [whole] * 2,
            out_specs=pl.BlockSpec((1, 3, tile, units), lambda i, s: (0, 0, i, 0)),
        ),
        compiler_params=pltpu.CompilerParams(vmem_limit_bytes=16 << 20),
        cost_estimate=cost(0.1),
    )(upper, x_mine, x_other, g_mine, g_other, m_mine, m_other, m_mine, m_other, *acts)


def permute_members(value, move):
    width = lax.axis_size("expert")
    pairs = []
    for source in range(width):
        group, member = divmod(source, GROUP)
        chip, core = divmod(member, CORES)
        chip, core = move(chip, core)
        pairs.append((source, group * GROUP + chip % CHIPS * CORES + core))
    return lax.ppermute(value, "expert", pairs)


def outward(value):
    return permute_members(value, lambda chip, core: (chip + 1 - 2 * core, core))


def inward(value):
    return permute_members(value, lambda chip, core: (chip - 1 + 2 * core, core))


def across(value):
    return permute_members(value, lambda chip, core: (chip + 2, core))


def other_core(value):
    return permute_members(value, lambda chip, core: (chip, 1 - core))


def mirror(value):
    count = lax.axis_size("pipe")
    return lax.ppermute(value, "pipe", [(k, count - 1 - k) for k in range(count)])


def across_groups(value):
    width = lax.axis_size("expert")
    groups = [[e * GROUP + g for e in range(width // GROUP)] for g in range(GROUP)]
    return lax.all_to_all(
        value, "expert", split_axis=0, concat_axis=0, axis_index_groups=groups, tiled=True
    )


def after(value, *others):
    return lax.optimization_barrier((value, *others))[0]


def across_sections(value):
    width, count = lax.axis_size("expert"), lax.axis_size("pipe")
    groups = [
        [section * width + e * GROUP + g for section in (k, count - 1 - k) for e in range(width // GROUP)]
        for k in range(count // 2)
        for g in range(GROUP)
    ]
    return lax.all_to_all(
        value, ("pipe", "expert"), split_axis=0, concat_axis=0, axis_index_groups=groups, tiled=True
    )


def pack(*pieces, us=1.0):
    rows, features = pieces[0].shape
    return run(pack_kernel, [((len(pieces) * rows, features), BF16)], *pieces, limit=2, us=us)[0]


def together(*values):
    return lax.optimization_barrier(values)


def body(tokens, out_grad, probs, expert_ids, w_gate, w_up, w_down):
    in_flight = lax.axis_size("expert") // GROUP
    features = tokens.shape[1]
    units = w_gate.shape[2]
    slots = in_flight * CAP
    upper = (lax.axis_index("pipe") >= lax.axis_size("pipe") // 2).astype(jnp.int32)
    upper = upper.reshape(1)
    rows = ((slots, features), BF16)
    x_rows, sent, select = run(
        route_kernel,
        [rows, ((2 * slots, features), BF16), ((tokens.shape[0], slots), BF16)],
        upper,
        tokens,
        out_grad,
        probs,
        expert_ids,
        scalars=1,
    )
    x_here = across_groups(x_rows)
    arrived = across_sections(after(sent, x_here))
    x_near, x_next = together(outward(x_here), inward(x_here))
    x_far = outward(x_near)
    arrived = after(arrived, x_near, x_next, x_far)
    g_here, m_here = run(split_kernel, [rows] * 2, upper, arrived, scalars=1, limit=2)
    x_mine = pack(x_here, x_near, x_next, x_far)
    x_other = other_core(x_mine)
    g_near, g_next, _ = together(outward(g_here), inward(g_here), x_mine)
    g_far = outward(g_near)
    gate_shape = ((2 * x_mine.shape[0], units), F32)
    gate, up = run(up_kernel, [gate_shape] * 2, x_mine, x_other, w_gate, w_up, us=3.0)
    g_far = after(g_far, gate)
    g_mine = pack(g_here, g_near, g_next, g_far)
    g_other = other_core(g_mine)

    m_here = after(m_here, g_far)
    m_near, m_next = outward(m_here), inward(m_here)
    acts_shape = ((3, gate.shape[0], units), BF16)
    acts = run(back_kernel, [acts_shape], g_mine, g_other, w_down, gate, up, us=3.0)[0]
    m_acts = mirror(acts)
    ready, m_near = together(acts, m_near)
    part = run(row_other_kernel, [(x_other.shape, BF16)], ready, w_gate, w_up, limit=14)[0]
    part = other_core(part)
    own, near, next_, far = run(
        row_mine_kernel, [(rows[0], F32), rows, rows, rows], ready, w_gate, w_up, part, limit=14
    )
    near, next_, far, m_far = together(
        inward(near), outward(next_), across(far), outward(m_near)
    )
    total = run(total_kernel, [rows], own, near, next_, far)[0]
    m_far, m_next, m_acts, _ = together(m_far, m_next, m_acts, total)
    m_mine = pack(m_here, m_near, m_next, m_far, us=10.0)
    m_other = pack(*(other_core(piece) for piece in (m_here, m_near, m_next, m_far)))
    returned = across_groups(total)
    weight_grads = weight_grads_of(
        upper, x_mine, x_other, g_mine, g_other, m_mine, m_other, acts, m_acts
    )
    returned, weight_grads = together(returned, weight_grads)
    tokens_grad = run(tokens_kernel, [(tokens.shape, BF16)], select, returned)[0]
    return (tokens_grad, weight_grads)


def solution(mesh):
    return jax.shard_map(
        body,
        mesh=mesh,
        in_specs=(
            P(("pipe", "expert"), None),
            P(("pipe", "expert"), None),
            P(("pipe", "expert"), None),
            P(("pipe", "expert"), None),
            P("pipe", None, "expert"),
            P("pipe", None, "expert"),
            P("pipe", "expert", None),
        ),
        out_specs=(P(("pipe", "expert"), None), P("pipe", None, None, "expert")),
        check_vma=False,
    )
```
